32 devices in a mesh: sec: 4 (over y, x), pen: 4 (over z), rhs: 2 (over core).
Axes of the slice: x: 2, y: 2, z: 4, core: 2. Of those that a mesh axis runs over, the one named last changes fastest.
Arguments:
- source: float32 [2, 4, 4, 128, 512], P(None, 'rhs', 'sec', None, 'pen'), may hold values from -8 to 8
- medium: float32 [4, 128, 512], P('sec', None, 'pen'), may hold values from 0 to 0.5
- damping: float32 [4, 128, 512], P('sec', None, 'pen'), may hold values from 0.05 to 0.8
- inv_x: float32 [4, 1], P('sec'), as said below
- inv_y: float32 [1, 128, 128], replicated, as said below
- inv_z: float32 [2, 256, 256], replicated, as said below
Outputs:
- solution: float32 [2, 4, 4, 128, 512], P(None, 'rhs', 'sec', None, 'pen')
The draws below stay inside these ranges and needn't reach their ends.
Inputs may be any that keep to these rules, and one draw needn't show every extreme that they name: Each entry of inv_x (one per section, since a section has 1 layer) is near 0.5: 0.5 plus a small random term. `inv_y`: each block is 0.5 times the identity plus dense off-diagonal terms. `inv_z`: each block is 0.5 times the identity plus dense off-diagonal terms.
All inputs are finite; a program needn't handle non-finite values.
Results may differ from the reference program's by a relative error of at most 0.0001.
Values sent between devices are 32-bit elements; how exact they have to be, the bound alone decides.
No kernel may reach another device: no remote copies, remote signals or barrier semaphores. Data moves between devices by JAX's collectives and lax.ppermute only.
A program may use at most 64 MiB of HBM per device.

```python
import math
import jax
import jax.numpy as jnp
from jax import lax

LX = 1
Y = 128
ITERS = 3
BY = 128
BZ = 256
NX = 4
NZ = 512
RHS = 4
NYB = 1
NZB = 2
N_SEC = 4


def make_blocks(key, count, length, spread):
    noise = jax.random.normal(key, (count, length, length), jnp.float32)
    ident = jnp.eye(length, dtype=jnp.float32)[None]
    return 0.5 * ident + spread * noise / jnp.sqrt(jnp.float32(length))


def draw_inv_x(key, part):
    blocks = make_blocks(jax.random.fold_in(key, 11), NX // LX, LX, 0.15)
    return blocks.reshape(NX, LX)


def draw_inv_y(key, part):
    return make_blocks(jax.random.fold_in(key, 12), NYB, BY, 0.3)


def draw_inv_z(key, part):
    return make_blocks(jax.random.fold_in(key, 13), NZB, BZ, 0.3)


def level_of(own_key, dims, cuts, least, largest):
    gain, own = 1.0, jax.random.fold_in(own_key, 6)
    for dim, parts in cuts:
        steps = jnp.exp(jax.random.uniform(jax.random.fold_in(own, dim), (parts,), jnp.float32, least / len(cuts), largest / len(cuts)))
        gain = gain * jnp.repeat(steps, dims[dim] // parts).reshape([-1 if axis == dim else 1 for axis in range(len(dims))])
    return gain


def scatter_about(stream_key, dims, scale, most, shards=(), kind=jnp.bfloat16):
    values = jax.random.normal(stream_key, dims, jnp.float32) * scale
    if len(shards) > 0:
        values = level_of(stream_key, dims, shards, -0.22, 0.18) * values
    return jnp.clip(values, min=-most, max=most).astype(kind)


def setup_inputs(seed: int = 0) -> dict:
    key_of = jax.random.split(jax.random.key(seed), 7)
    source = scatter_about(key_of[0], (2, RHS, NX, Y, NZ), 1.0, 8.0, ((1, 2), (2, 4), (4, 4)), jnp.float32)
    medium = jnp.clip(0.5 * jax.random.uniform(key_of[1], (NX, Y, NZ), jnp.float32) ** level_of(key_of[1], (NX, Y, NZ), ((0, 4), (2, 4)), -0.2, 0.2), 0.0, 0.5)
    damping = jnp.clip(jnp.exp(math.log(0.8) - 2.7725887 * jax.random.uniform(key_of[2], (NX, Y, NZ), jnp.float32) ** level_of(key_of[2], (NX, Y, NZ), ((0, 4), (2, 4)), -0.2, 0.2)), 0.05, 0.8)
    inv_x = draw_inv_x(jax.random.fold_in(key_of[6], 71), 0)
    inv_y = draw_inv_y(jax.random.fold_in(key_of[6], 71), 0)
    inv_z = draw_inv_z(jax.random.fold_in(key_of[6], 71), 0)
    return dict(source=source, medium=medium, damping=damping, inv_x=inv_x, inv_y=inv_y, inv_z=inv_z)


def weight(off_x, off_y, off_z):
    reach = abs(off_x) + abs(off_y) + abs(off_z)
    if reach == 1:
        if off_x == -1:
            return 0.14
        if off_x == 1:
            return 0.06
        return 0.1
    if reach == 2:
        return 0.03
    return 0.01


def apply_op(field, padded, medium, damping):
    layers, columns, depth = field.shape[2], field.shape[3], field.shape[4]
    nearby = jnp.zeros_like(field)
    for off_x in (-1, 0, 1):
        for off_y in (-1, 0, 1):
            for off_z in (-1, 0, 1):
                if off_x == 0 and off_y == 0 and off_z == 0:
                    continue
                piece = padded[:, :, 1 + off_x:1 + off_x + layers, 1 + off_y:1 + off_y + columns, 1 + off_z:1 + off_z + depth]
                nearby = nearby + weight(off_x, off_y, off_z) * piece
    real_shift = 1.3 + medium
    real_part = real_shift * field[0] - damping * field[1] - nearby[0]
    imag_part = real_shift * field[1] + damping * field[0] - nearby[1]
    return jnp.stack([real_part, imag_part])


def residual(forcing, field, trace_in, medium, damping):
    blank = jnp.zeros_like(trace_in)[:, :, None]
    full = jnp.concatenate([trace_in[:, :, None], field, blank], axis=2)
    full = jnp.pad(full, ((0, 0), (0, 0), (0, 0), (1, 1), (1, 1)))
    return forcing - apply_op(field, full, medium, damping)


def solve_x(residue, blocks):
    return jnp.einsum('ij,prjyz->priyz', blocks, residue, precision=lax.Precision.HIGHEST)


def solve_y(residue, blocks):
    shape = residue.shape
    split = residue.reshape(shape[0], shape[1], shape[2], blocks.shape[0], blocks.shape[1], shape[4])
    done = jnp.einsum('bij,prxbjz->prxbiz', blocks, split, precision=lax.Precision.HIGHEST)
    return done.reshape(shape)


def solve_z(residue, blocks):
    shape = residue.shape
    split = residue.reshape(shape[:4] + (blocks.shape[0], blocks.shape[1]))
    done = jnp.einsum('bij,prxybj->prxybi', blocks, split, precision=lax.Precision.HIGHEST)
    return done.reshape(shape)


def reference(source, medium, damping, inv_x, inv_y, inv_z):
    trace_in = jnp.zeros((2, source.shape[1], source.shape[3], source.shape[4]), jnp.float32)
    results = []
    for section in range(N_SEC):
        lower = section * LX
        forcing = source[:, :, lower:lower + LX]
        med_part = medium[lower:lower + LX]
        damp_part = damping[lower:lower + LX]
        x_blocks = inv_x[lower:lower + LX]
        field = jnp.zeros_like(forcing)
        for sweep in range(ITERS):
            field = field + solve_x(residual(forcing, field, trace_in, med_part, damp_part), x_blocks)
            field = field + solve_y(residual(forcing, field, trace_in, med_part, damp_part), inv_y)
            field = field + solve_z(residual(forcing, field, trace_in, med_part, damp_part), inv_z)
        results.append(field)
        trace_in = field[:, :, -1]
    return jnp.concatenate(results, axis=2)
```

```python
import functools

import jax
import jax.numpy as jnp
from jax import lax
from jax.experimental import pallas as pl
from jax.experimental.pallas import tpu as pltpu
from jax.sharding import PartitionSpec as P

ITERS = 3
ROWS = 16
PAD = 8
F32, BF16 = jnp.float32, jnp.bfloat16


def halves(value):
    high = value.astype(BF16)
    return high, (value - high.astype(F32)).astype(BF16)


def split(value):
    high = lax.reduce_precision(value, exponent_bits=8, mantissa_bits=7)
    return high.astype(BF16), (value - high).astype(BF16)


def dot(a, b):
    return jnp.dot(a, b, preferred_element_type=F32)


def filtered(pieces, ratio, first, last):
    count = len(pieces)
    lanes = pieces[0].shape[1]
    up = [pltpu.roll(piece, 1, 1) for piece in pieces]
    down = [pltpu.roll(piece, lanes - 1, 1) for piece in pieces]
    zero = jnp.zeros_like(pieces[0])
    out = []
    for q in range(count):
        left = jnp.where(first, up[q - 1] if q > 0 else zero, up[q])
        right = jnp.where(last, down[q + 1] if q + 1 < count else zero, down[q])
        out.append(pieces[q] + ratio * (left + right))
    return out


def section_kernel(
    place, mine, other, trace, y_left, z_high, z_low, out, res, step, diag, y_in, zh_in, zl_in
):
    parts, quarters, height, lanes = 2, res.shape[0], diag.shape[2], res.shape[2]
    y_blocks, y_size = y_left.shape[0], y_left.shape[1] // 2
    per_block = z_high.shape[1] // lanes
    chunks = height // ROWS
    lane = lax.broadcasted_iota(jnp.int32, (ROWS, lanes), 1)
    first, last = lane == 0, lane == lanes - 1
    has_source = place[0] == 1
    gain = jnp.where(has_source, mine[0, 2 * height, :], other[0, 2 * height, :])[None, :]

    pads = jnp.zeros((PAD, lanes), F32)
    for buffer in range(2):
        for q in range(quarters):
            for c in range(parts):
                step[buffer, q, c, :PAD] = pads
                step[buffer, q, c, PAD + height :] = pads

    def neighbours(read, base, ratio):
        tall = [
            read(q, base) + ratio * (read(q, base - 1) + read(q, base + 1))
            for q in range(quarters)
        ]
        return filtered(tall, ratio, first, last)

    def emit(q, c, base, value):
        res[q, pl.ds(c * height + base, ROWS)] = value
        high, low = halves(value)
        return high, low

    for c in range(parts):
        for q in range(quarters):
            step[1, q, c, PAD : PAD + height] = trace[q, c * height : (c + 1) * height]

    def start(i, carry):
        base = pl.multiple_of(i * ROWS, ROWS)
        for c in range(parts):
            rows = pl.ds(c * height + base, ROWS)
            near = neighbours(
                lambda q, b: step[1, q, c, pl.ds(PAD + b, ROWS)], base, 1.0 / 3.0
            )
            for d in range(quarters):
                q = place[1 + d]
                a, b = mine[d, rows], other[d, rows]
                res[q, rows] = jnp.where(has_source, a, b)
                diag[q, c, pl.ds(base, ROWS)] = jnp.where(has_source, b, a) + (
                    1.3 + 1.0 / 3.0 if c == 0 else 0.0
                )
            for q in range(quarters):
                value = res[q, rows] + 0.09 * near[q] + 0.05 * trace[q, rows]
                res[q, rows] = value
                step[0, q, c, pl.ds(PAD + base, ROWS)] = gain * value
                out[q, rows] = jnp.zeros_like(value)
        return carry

    lax.fori_loop(0, chunks, start, 0)

    def apply(source, then):
        def chunk(i, carry):
            base = pl.multiple_of(i * ROWS, ROWS)
            near = [
                neighbours(
                    lambda q, b: step[source, q, c, pl.ds(PAD + b, ROWS)], base, 0.3
                )
                for c in range(parts)
            ]
            for q in range(quarters):
                du = [step[source, q, c, pl.ds(PAD + base, ROWS)] for c in range(parts)]
                real, imag = (diag[q, c, pl.ds(base, ROWS)] for c in range(parts))
                turned = [real * du[0] - imag * du[1], real * du[1] + imag * du[0]]
                for c in range(parts):
                    rows = pl.ds(c * height + base, ROWS)
                    out[q, rows] += du[c]
                    value = res[q, rows] - turned[c] + (1.0 / 3.0) * near[c][q]
                    res[q, rows] = value
                    then(q, c, base, rows, value)
            return carry

        lax.fori_loop(0, chunks, chunk, 0)

    def for_y(q, c, base, rows, value):
        high, low = halves(value)
        y_in[q, c, 0, pl.ds(base, ROWS)] = high
        y_in[q, c, 1, pl.ds(base, ROWS)] = low

    def for_z(q, c, base, rows, value):
        zh_in[q, rows], zl_in[q, rows] = halves(value)

    def for_x(q, c, base, rows, value):
        step[0, q, c, pl.ds(PAD + base, ROWS)] = gain * value

    def solve_y():
        for b in range(y_blocks):
            rows = slice(b * y_size, (b + 1) * y_size)
            for c in range(parts):
                for q in range(0, quarters, per_block):
                    both = jnp.concatenate(
                        [
                            jnp.concatenate([y_in[q + k, c, h, rows] for h in range(2)], axis=0)
                            for k in range(per_block)
                        ],
                        axis=1,
                    )
                    done = dot(y_left[b], both)
                    done = done[:y_size] + done[y_size:]
                    for k in range(per_block):
                        step[1, q + k, c, PAD + b * y_size : PAD + (b + 1) * y_size] = done[
                            :, k * lanes : (k + 1) * lanes
                        ]

    def solve_z(add):
        for b in range(quarters // per_block):
            at = range(b * per_block, (b + 1) * per_block)
            high = jnp.concatenate([zh_in[q] for q in at], axis=1)
            low = jnp.concatenate([zl_in[q] for q in at], axis=1)
            done = dot(high, z_low[b]) + dot(low, z_high[b]) + dot(high, z_high[b])
            for k, q in enumerate(at):
                piece = done[:, k * lanes : (k + 1) * lanes]
                if add:
                    out[q] += piece
                else:
                    for c in range(parts):
                        step[1, q, c, PAD : PAD + height] = piece[
                            c * height : (c + 1) * height
                        ]

    def sweep(i, carry):
        apply(0, for_y)
        solve_y()
        apply(1, for_z)

        @pl.when(i + 1 < ITERS)
        def _():
            solve_z(False)
            apply(1, for_x)

        return carry

    lax.fori_loop(0, ITERS, sweep, 0)
    solve_z(True)


def section(place, mine, other, trace, y_left, z_high, z_low):
    quarters, rows, lanes = trace.shape
    height = rows // 2
    vmem, smem = (pl.BlockSpec(memory_space=space) for space in (pltpu.VMEM, pltpu.SMEM))
    return pl.pallas_call(
        section_kernel,
        out_shape=jax.ShapeDtypeStruct(trace.shape, F32),
        in_specs=[smem] + [vmem] * 6,
        out_specs=vmem,
        scratch_shapes=[
            pltpu.VMEM((quarters, rows, lanes), F32),
            pltpu.VMEM((2, quarters, 2, height + 2 * PAD, lanes), F32),
            pltpu.VMEM((quarters, 2, height, lanes), F32),
            pltpu.VMEM((quarters, 2, 2, height, lanes), BF16),
            pltpu.VMEM((quarters, rows, lanes), BF16),
            pltpu.VMEM((quarters, rows, lanes), BF16),
        ],
    )(place, mine, other, trace, y_left, z_high, z_low)


def local(source, medium, damping, inv_x, inv_y, inv_z):
    rhs, _, height, lanes = source.shape[1:]
    sections, chips, cores = (lax.axis_size(a) for a in ("sec", "pen", "rhs"))
    pen, core = lax.axis_index("pen"), lax.axis_index("rhs")
    total = rhs * cores

    def owner(chip):
        return (chip % total) // rhs

    options = jnp.concatenate(
        [source[:, :, 0].swapaxes(0, 1), jnp.concatenate([medium, damping])[None]]
    ).reshape(rhs + 1, 2 * height, lanes)
    scale = jnp.broadcast_to(inv_x, (8, lanes))

    def message(distance):
        target = pen ^ distance
        pick = jnp.where(owner(target) == core, (target % total) % rhs, rhs)
        body = lax.dynamic_index_in_dim(options, pick, keepdims=False)
        return jnp.concatenate([body, scale])

    gathered = [message(0)] + [
        lax.ppermute(message(d), "pen", [(i, i ^ d) for i in range(chips)])
        for d in range(1, chips)
    ]
    own = jnp.stack(gathered)

    y_high, y_low = split(inv_y)
    y_left = jnp.concatenate(
        [jnp.concatenate([y_high, y_high], axis=2), jnp.concatenate([y_low, y_low], axis=2)],
        axis=1,
    )
    z_high, z_low = split(inv_z.swapaxes(1, 2))
    place = jnp.concatenate(
        [
            jnp.where(owner(pen) == core, 1, 0)[None],
            pen ^ jnp.arange(chips, dtype=jnp.int32),
        ]
    ).astype(jnp.int32)
    swap = [(i, (i + 1) % cores) for i in range(cores)]
    fields = jnp.zeros((chips, 2 * height, lanes), F32)
    received = [
        lax.ppermute(own, "sec", [(j, j + k) for j in range(sections - k)])
        for k in range(sections - 1, 0, -1)
    ] + [own]
    for mine in received:
        other = lax.ppermute(mine, "rhs", swap)
        fields = section(place, mine, other, fields, y_left, z_high, z_low)

    def piece(at):
        return lax.dynamic_index_in_dim(fields, at, keepdims=False)

    def device(chip, which):
        return chip * cores + which

    result = jnp.zeros((rhs, 2 * height, lanes), F32)
    for d in range(total):
        pairs = [(device(i, owner(i)), device(i ^ d, owner(i))) for i in range(chips)]
        got = piece(pen ^ d)
        if d > 0:
            got = lax.ppermute(got, ("pen", "rhs"), pairs)
        origin = (pen ^ d) % total
        slot = (jnp.arange(rhs)[:, None, None] == origin % rhs) & (origin // rhs == core)
        result = jnp.where(slot, got[None], result)
    return result.reshape(rhs, 2, height, lanes).swapaxes(0, 1)[:, :, None]


def solution(mesh):
    return jax.shard_map(
        local,
        mesh=mesh,
        in_specs=(
            P(None, "rhs", "sec", None, "pen"),
            P("sec", None, "pen"),
            P("sec", None, "pen"),
            P("sec", None),
            P(),
            P(),
        ),
        out_specs=P(None, "rhs", "sec", None, "pen"),
        check_vma=False,
    )
```

```python
import functools

import jax
import jax.numpy as jnp
from jax import lax
from jax.experimental import pallas as pl
from jax.experimental.pallas import tpu as pltpu
from jax.sharding import PartitionSpec as P

ITERS = 3
ROWS = 16
SPARE = 2**22
PAD = 8
F32, BF16 = jnp.float32, jnp.bfloat16

CORNER, C, CENTRE = 0.03, 10.0 / 3.0, 1.0 / 3.0
UP, UP_REST = 0.01, 0.05


def halves(value):
    high = value.astype(BF16)
    return high, (value - high.astype(F32)).astype(BF16)


def split(value):
    high = lax.reduce_precision(value, exponent_bits=8, mantissa_bits=7)
    return high.astype(BF16), (value - high).astype(BF16)


def dot(a, b):
    return jnp.dot(a, b, preferred_element_type=F32)


def section_kernel(count, place, *refs):
    pieces, refs = refs[: 2 * count * 2], refs[2 * count * 2 :]
    trace, y_left, z_high, z_low, out, res, step, diag, y_in, zh_in, zl_in = refs
    parts, quarters, height, lanes = 2, res.shape[0], diag.shape[2], res.shape[2]
    y_blocks, y_size = y_left.shape[0], y_left.shape[1] // 2
    per_block = z_high.shape[1] // lanes
    chunks = height // ROWS
    lane = lax.broadcasted_iota(jnp.int32, (ROWS, lanes), 1)
    first, last = lane == 0, lane == lanes - 1

    pads = jnp.zeros((PAD, lanes), F32)
    for buffer in range(2):
        for q in range(quarters):
            for c in range(parts):
                step[buffer, q, c, :PAD] = pads
                step[buffer, q, c, PAD + height :] = pads

    def neighbours(buffer, c, base, weight):
        tall = []
        for q in range(quarters):
            here = step[buffer, q, c, pl.ds(PAD + base, ROWS)]
            above = step[buffer, q, c, pl.ds(PAD + base - 1, ROWS)]
            below = step[buffer, q, c, pl.ds(PAD + base + 1, ROWS)]
            tall.append(weight * here + (above + below))
        up = [pltpu.roll(piece, 1, 1) for piece in tall]
        down = [pltpu.roll(piece, lanes - 1, 1) for piece in tall]
        near = []
        for q in range(quarters):
            left = jnp.where(first, up[q - 1] if q > 0 else 0.0, up[q])
            right = jnp.where(last, down[q + 1] if q + 1 < quarters else 0.0, down[q])
            near.append(weight * tall[q] + (left + right))
        return near

    def over_chunks(body):
        def chunk(i, carry):
            body(pl.multiple_of(i * ROWS, ROWS))
            return carry

        lax.fori_loop(0, chunks, chunk, 0, unroll=True)

    def at(arrays, d):
        size = arrays[0].shape[0]
        return arrays[d // size], d % size

    def load(source, diagonal, before, gain):
        for q in range(quarters):
            for c in range(parts):
                step[1, q, c, PAD : PAD + height] = before[q, c * height : (c + 1) * height]
        for d in range(quarters):
            q = place[d]
            array, k = at(source, d)
            res[q] = array[k, : parts * height] * (1.0 / CORNER)
            array, k = at(diagonal, d)
            diag[q, 0] = array[k, :height] * (1.0 / CORNER) + (1.3 + CENTRE) / CORNER
            diag[q, 1] = array[k, height : 2 * height] * (1.0 / CORNER)

        def body(base):
            for c in range(parts):
                rows = pl.ds(c * height + base, ROWS)
                near = neighbours(1, c, base, 3.0)
                for q in range(quarters):
                    here = step[1, q, c, pl.ds(PAD + base, ROWS)]
                    value = res[q, rows] + (UP / CORNER) * near[q] + (UP_REST / CORNER) * here
                    res[q, rows] = value
                    step[0, q, c, pl.ds(PAD + base, ROWS)] = gain * value

        over_chunks(body)

    def apply(source, add, then):
        def body(base):
            near = [neighbours(source, c, base, C) for c in range(parts)]
            for q in range(quarters):
                du = [step[source, q, c, pl.ds(PAD + base, ROWS)] for c in range(parts)]
                real, imag = (diag[q, c, pl.ds(base, ROWS)] for c in range(parts))
                turned = [real * du[0] - imag * du[1], real * du[1] + imag * du[0]]
                for c in range(parts):
                    rows = pl.ds(c * height + base, ROWS)
                    if add is not None:
                        out[q, rows] = add(q, c, base, rows, du[c])
                    value = res[q, rows] - turned[c] + near[c][q]
                    res[q, rows] = value
                    then(q, c, base, rows, value)

        over_chunks(body)

    def for_y(q, c, base, rows, value):
        high, low = halves(value)
        y_in[q, c, 0, pl.ds(base, ROWS)] = high
        y_in[q, c, 1, pl.ds(base, ROWS)] = low

    def for_z(q, c, base, rows, value):
        zh_in[q, rows], zl_in[q, rows] = halves(value)

    def solve_y():
        for b in range(y_blocks):
            rows = slice(b * y_size, (b + 1) * y_size)
            for c in range(parts):
                for q in range(0, quarters, per_block):
                    both = jnp.concatenate(
                        [
                            jnp.concatenate([y_in[q + k, c, h, rows] for h in range(2)], axis=0)
                            for k in range(per_block)
                        ],
                        axis=1,
                    )
                    done = dot(y_left[b], both)
                    done = done[:y_size] + done[y_size:]
                    for k in range(per_block):
                        step[1, q + k, c, PAD + b * y_size : PAD + (b + 1) * y_size] = done[
                            :, k * lanes : (k + 1) * lanes
                        ]

    def solve_z(add):
        for b in range(quarters // per_block):
            span = range(b * per_block, (b + 1) * per_block)
            high = jnp.concatenate([zh_in[q] for q in span], axis=1)
            low = jnp.concatenate([zl_in[q] for q in span], axis=1)
            done = dot(high, z_low[b]) + dot(low, z_high[b]) + dot(high, z_high[b])
            for k, q in enumerate(span):
                piece = done[:, k * lanes : (k + 1) * lanes]
                if add:
                    out[q] += piece
                else:
                    for c in range(parts):
                        step[1, q, c, PAD : PAD + height] = piece[
                            c * height : (c + 1) * height
                        ]

    for index in range(count):
        mine = pieces[4 * index : 4 * index + 4]
        gain = CORNER * mine[0][0, 2 * height, :][None, :]
        load(mine[:2], mine[2:], trace if index == 0 else out, gain)
        for q in range(quarters):
            out[q] = jnp.zeros(out.shape[1:], F32)

        def for_x(q, c, base, rows, value):
            step[0, q, c, pl.ds(PAD + base, ROWS)] = gain * value

        def two_steps(q, c, base, rows, du):
            return out[q, rows] + (step[0, q, c, pl.ds(PAD + base, ROWS)] + du)

        def one_step(q, c, base, rows, du):
            return out[q, rows] + du

        def sweep(i, carry):
            apply(0, None, for_y)
            solve_y()
            apply(1, two_steps, for_z)

            @pl.when(i + 1 < ITERS)
            def _():
                solve_z(False)
                apply(1, one_step, for_x)

            return carry

        lax.fori_loop(0, ITERS, sweep, 0)
        solve_z(True)


def solve_sections(place, pieces, trace, y_left, z_high, z_low):
    quarters, rows, lanes = trace.shape
    height = rows // 2
    vmem, smem = (pl.BlockSpec(memory_space=space) for space in (pltpu.VMEM, pltpu.SMEM))
    flat = [array for four in pieces for array in four]
    count = len(pieces)
    scratch = [
        pltpu.VMEM((quarters, rows, lanes), F32),
        pltpu.VMEM((2, quarters, 2, height + 2 * PAD, lanes), F32),
        pltpu.VMEM((quarters, 2, height, lanes), F32),
        pltpu.VMEM((quarters, 2, 2, height, lanes), BF16),
        pltpu.VMEM((quarters, rows, lanes), BF16),
        pltpu.VMEM((quarters, rows, lanes), BF16),
    ]
    inputs = flat + [trace, y_left, z_high, z_low]
    held = sum(a.size * a.dtype.itemsize for a in inputs + [trace])
    held += 8 * trace.size * trace.dtype.itemsize
    return pl.pallas_call(
        functools.partial(section_kernel, count),
        out_shape=jax.ShapeDtypeStruct(trace.shape, F32),
        in_specs=[smem] + [vmem] * (len(flat) + 4),
        out_specs=vmem,
        scratch_shapes=scratch,
        compiler_params=pltpu.CompilerParams(vmem_limit_bytes=held + SPARE),
        name=f"sections_{count}",
    )(place, *flat, trace, y_left, z_high, z_low)


def local(source, medium, damping, inv_x, inv_y, inv_z):
    rhs, _, height, lanes = source.shape[1:]
    sections, chips, cores = (lax.axis_size(a) for a in ("sec", "pen", "rhs"))
    pen, core = lax.axis_index("pen"), lax.axis_index("rhs")
    total = rhs * cores

    def owner(chip):
        return (chip % total) // rhs

    options = jnp.concatenate(
        [source[:, :, 0].swapaxes(0, 1), jnp.concatenate([medium, damping])[None]]
    ).reshape(rhs + 1, 2 * height, lanes)
    scale = jnp.broadcast_to(inv_x, (8, lanes))

    def message(distance):
        target = pen ^ distance
        pick = jnp.where(owner(target) == core, (target % total) % rhs, rhs)
        body = lax.dynamic_index_in_dim(options, pick, keepdims=False)
        return jnp.concatenate([body, scale])

    def between(value, down, from_owner):
        pairs = []
        for j in range(sections - down):
            for p in range(chips):
                here = owner(p) if from_owner else (owner(p) + 1) % cores
                pairs.append(
                    (
                        (j * chips + p) * cores + here,
                        ((j + down) * chips + p) * cores + owner(p),
                    )
                )
        return lax.ppermute(value, ("sec", "pen", "rhs"), pairs)

    got = [message(0)] + [
        lax.ppermute(message(d), "pen", [(i, i ^ d) for i in range(chips)])
        for d in range(1, chips)
    ]
    own = [jnp.stack(got[: chips // 2]), jnp.stack(got[chips // 2 :])]

    y_high, y_low = split(CORNER * inv_y)
    y_left = jnp.concatenate(
        [jnp.concatenate([y_high, y_high], axis=2), jnp.concatenate([y_low, y_low], axis=2)],
        axis=1,
    )
    z_high, z_low = split(CORNER * inv_z.swapaxes(1, 2))
    place = pen ^ jnp.arange(chips, dtype=jnp.int32)

    arrived = {k: [None] * 4 for k in range(sections)}
    for half in range(2):
        for k in range(sections - 1, 0, -1):
            arrived[k][half] = between(own[half], k, True)
            arrived[k][2 + half] = between(own[half], k, False)
        arrived[0][half] = own[half]
        arrived[0][2 + half] = between(own[half], 0, False)

    fields = jnp.zeros((chips, 2 * height, lanes), F32)
    fields = solve_sections(
        place, [arrived[sections - 1]], fields, y_left, z_high, z_low
    )
    if sections > 1:
        rest = [arrived[k] for k in range(sections - 2, -1, -1)]
        fields = solve_sections(place, rest, fields, y_left, z_high, z_low)

    result = jnp.zeros((rhs, 2 * height, lanes), F32)
    for d in range(total):
        piece = lax.dynamic_index_in_dim(fields, pen ^ d, keepdims=False)
        if d > 0:
            pairs = [
                (i * cores + owner(i), (i ^ d) * cores + owner(i)) for i in range(chips)
            ]
            piece = lax.ppermute(piece, ("pen", "rhs"), pairs)
        origin = (pen ^ d) % total
        slot = (jnp.arange(rhs)[:, None, None] == origin % rhs) & (origin // rhs == core)
        result = jnp.where(slot, piece[None], result)
    return result.reshape(rhs, 2, height, lanes).swapaxes(0, 1)[:, :, None]


def solution(mesh):
    return jax.shard_map(
        local,
        mesh=mesh,
        in_specs=(
            P(None, "rhs", "sec", None, "pen"),
            P("sec", None, "pen"),
            P("sec", None, "pen"),
            P("sec", None),
            P(),
            P(),
        ),
        out_specs=P(None, "rhs", "sec", None, "pen"),
        check_vma=False,
    )
```

```python
import functools

import jax
import jax.numpy as jnp
from jax import lax
from jax.experimental import pallas as pl
from jax.experimental.pallas import tpu as pltpu
from jax.sharding import PartitionSpec as P


ITERS = 3
ROWS = 16
SPARE = 2**22
PAD = 8
F32, BF16 = jnp.float32, jnp.bfloat16

CORNER, C, CENTRE = 0.03, 10.0 / 3.0, 1.0 / 3.0
UP, UP_REST = 0.01, 0.05


def halves(value):
    high = value.astype(BF16)
    return high, (value - high.astype(F32)).astype(BF16)


def split(value):
    high = lax.reduce_precision(value, exponent_bits=8, mantissa_bits=7)
    return high.astype(BF16), (value - high).astype(BF16)


def dot(a, b):
    return jnp.dot(a, b, preferred_element_type=F32)


def section_kernel(parted, place, *refs):
    refs = list(refs)
    pieces = [[[refs.pop(0) for _ in range(n)] for _ in range(2)] for n in parted]
    trace, y_left, z_high, z_low, out, res, step, diag, y_in, zh_in, zl_in = refs
    parts, quarters, height, lanes = 2, res.shape[0], diag.shape[2], res.shape[2]
    y_blocks, y_size = y_left.shape[0], y_left.shape[1] // 2
    per_block = z_high.shape[1] // lanes
    chunks = height // ROWS
    lane = lax.broadcasted_iota(jnp.int32, (ROWS, lanes), 1)
    first, last = lane == 0, lane == lanes - 1

    pads = jnp.zeros((PAD, lanes), F32)
    for buffer in range(2):
        for q in range(quarters):
            for c in range(parts):
                step[buffer, q, c, :PAD] = pads
                step[buffer, q, c, PAD + height :] = pads

    def neighbours(buffer, c, base, weight):
        tall = []
        for q in range(quarters):
            here = step[buffer, q, c, pl.ds(PAD + base, ROWS)]
            above = step[buffer, q, c, pl.ds(PAD + base - 1, ROWS)]
            below = step[buffer, q, c, pl.ds(PAD + base + 1, ROWS)]
            tall.append(weight * here + (above + below))
        up = [pltpu.roll(piece, 1, 1) for piece in tall]
        down = [pltpu.roll(piece, lanes - 1, 1) for piece in tall]
        near = []
        for q in range(quarters):
            left = jnp.where(first, up[q - 1] if q > 0 else 0.0, up[q])
            right = jnp.where(last, down[q + 1] if q + 1 < quarters else 0.0, down[q])
            near.append(weight * tall[q] + (left + right))
        return near

    def over_chunks(body):
        def chunk(i, carry):
            body(pl.multiple_of(i * ROWS, ROWS))
            return carry

        lax.fori_loop(0, chunks, chunk, 0, unroll=True)

    def at(arrays, d):
        size = arrays[0].shape[0]
        return arrays[d // size], d % size

    def load(source, diagonal, before, gain):
        for q in range(quarters):
            for c in range(parts):
                step[1, q, c, PAD : PAD + height] = before[q, c * height : (c + 1) * height]
        for d in range(quarters):
            q = place[d]
            array, k = at(source, d)
            res[q] = array[k, : parts * height] * (1.0 / CORNER)
            array, k = at(diagonal, d)
            diag[q, 0] = array[k, :height] * (1.0 / CORNER) + (1.3 + CENTRE) / CORNER
            diag[q, 1] = array[k, height : 2 * height] * (1.0 / CORNER)

        def body(base):
            for c in range(parts):
                rows = pl.ds(c * height + base, ROWS)
                near = neighbours(1, c, base, 3.0)
                for q in range(quarters):
                    here = step[1, q, c, pl.ds(PAD + base, ROWS)]
                    value = res[q, rows] + (UP / CORNER) * near[q] + (UP_REST / CORNER) * here
                    res[q, rows] = value
                    step[0, q, c, pl.ds(PAD + base, ROWS)] = gain * value

        over_chunks(body)

    def apply(source, add, then):
        def body(base):
            near = [neighbours(source, c, base, C) for c in range(parts)]
            for q in range(quarters):
                du = [step[source, q, c, pl.ds(PAD + base, ROWS)] for c in range(parts)]
                real, imag = (diag[q, c, pl.ds(base, ROWS)] for c in range(parts))
                turned = [real * du[0] - imag * du[1], real * du[1] + imag * du[0]]
                for c in range(parts):
                    rows = pl.ds(c * height + base, ROWS)
                    if add is not None:
                        out[q, rows] = add(q, c, base, rows, du[c])
                    value = res[q, rows] - turned[c] + near[c][q]
                    res[q, rows] = value
                    then(q, c, base, rows, value)

        over_chunks(body)

    def for_y(q, c, base, rows, value):
        high, low = halves(value)
        y_in[q, c, 0, pl.ds(base, ROWS)] = high
        y_in[q, c, 1, pl.ds(base, ROWS)] = low

    def for_z(q, c, base, rows, value):
        zh_in[q, rows], zl_in[q, rows] = halves(value)

    def solve_y():
        for b in range(y_blocks):
            rows = slice(b * y_size, (b + 1) * y_size)
            for c in range(parts):
                for q in range(0, quarters, per_block):
                    both = jnp.concatenate(
                        [
                            jnp.concatenate([y_in[q + k, c, h, rows] for h in range(2)], axis=0)
                            for k in range(per_block)
                        ],
                        axis=1,
                    )
                    done = dot(y_left[b], both)
                    done = done[:y_size] + done[y_size:]
                    for k in range(per_block):
                        step[1, q + k, c, PAD + b * y_size : PAD + (b + 1) * y_size] = done[
                            :, k * lanes : (k + 1) * lanes
                        ]

    def solve_z(add):
        for b in range(quarters // per_block):
            span = range(b * per_block, (b + 1) * per_block)
            high = jnp.concatenate([zh_in[q] for q in span], axis=1)
            low = jnp.concatenate([zl_in[q] for q in span], axis=1)
            done = dot(high, z_low[b]) + dot(low, z_high[b]) + dot(high, z_high[b])
            for k, q in enumerate(span):
                piece = done[:, k * lanes : (k + 1) * lanes]
                if add:
                    out[q] += piece
                else:
                    for c in range(parts):
                        step[1, q, c, PAD : PAD + height] = piece[
                            c * height : (c + 1) * height
                        ]

    for index, (source, diagonal) in enumerate(pieces):
        gain = CORNER * source[0][0, 2 * height, :][None, :]
        load(source, diagonal, trace if index == 0 else out, gain)
        for q in range(quarters):
            out[q] = jnp.zeros(out.shape[1:], F32)

        def for_x(q, c, base, rows, value):
            step[0, q, c, pl.ds(PAD + base, ROWS)] = gain * value

        def two_steps(q, c, base, rows, du):
            return out[q, rows] + (step[0, q, c, pl.ds(PAD + base, ROWS)] + du)

        def one_step(q, c, base, rows, du):
            return out[q, rows] + du

        def sweep(i, carry):
            apply(0, None, for_y)
            solve_y()
            apply(1, two_steps, for_z)

            @pl.when(i + 1 < ITERS)
            def _():
                solve_z(False)
                apply(1, one_step, for_x)

            return carry

        lax.fori_loop(0, ITERS, sweep, 0)
        solve_z(True)


def solve_sections(place, pieces, trace, y_left, z_high, z_low):
    quarters, rows, lanes = trace.shape
    height = rows // 2
    vmem, smem = (pl.BlockSpec(memory_space=space) for space in (pltpu.VMEM, pltpu.SMEM))
    flat = [array for section in pieces for kind in section for array in kind]
    parted = tuple(len(source) for source, _ in pieces)
    scratch = [
        pltpu.VMEM((quarters, rows, lanes), F32),
        pltpu.VMEM((2, quarters, 2, height + 2 * PAD, lanes), F32),
        pltpu.VMEM((quarters, 2, height, lanes), F32),
        pltpu.VMEM((quarters, 2, 2, height, lanes), BF16),
        pltpu.VMEM((quarters, rows, lanes), BF16),
        pltpu.VMEM((quarters, rows, lanes), BF16),
    ]
    inputs = flat + [trace, y_left, z_high, z_low]
    held = sum(a.size * a.dtype.itemsize for a in inputs + [trace])
    held += 8 * trace.size * trace.dtype.itemsize
    return pl.pallas_call(
        functools.partial(section_kernel, parted),
        out_shape=jax.ShapeDtypeStruct(trace.shape, F32),
        in_specs=[smem] + [vmem] * (len(flat) + 4),
        out_specs=vmem,
        scratch_shapes=scratch,
        compiler_params=pltpu.CompilerParams(vmem_limit_bytes=held + SPARE),
    )(place, *flat, trace, y_left, z_high, z_low)


def local(source, medium, damping, inv_x, inv_y, inv_z):
    rhs, _, height, lanes = source.shape[1:]
    sections, chips, cores = (lax.axis_size(a) for a in ("sec", "pen", "rhs"))
    pen, core = lax.axis_index("pen"), lax.axis_index("rhs")
    total = rhs * cores

    def owner(chip):
        return (chip % total) // rhs

    options = jnp.concatenate(
        [source[:, :, 0].swapaxes(0, 1), jnp.concatenate([medium, damping])[None]]
    ).reshape(rhs + 1, 2 * height, lanes)
    scale = jnp.broadcast_to(inv_x, (8, lanes))

    def message(distance):
        target = pen ^ distance
        pick = jnp.where(owner(target) == core, (target % total) % rhs, rhs)
        body = lax.dynamic_index_in_dim(options, pick, keepdims=False)
        return jnp.concatenate([body, scale])

    def between(value, down, from_owner):
        pairs = []
        for j in range(sections - down):
            for p in range(chips):
                here = owner(p) if from_owner else (owner(p) + 1) % cores
                pairs.append(
                    (
                        (j * chips + p) * cores + here,
                        ((j + down) * chips + p) * cores + owner(p),
                    )
                )
        return lax.ppermute(value, ("sec", "pen", "rhs"), pairs)

    y_high, y_low = split(CORNER * inv_y)
    y_left = jnp.concatenate(
        [jnp.concatenate([y_high, y_high], axis=2), jnp.concatenate([y_low, y_low], axis=2)],
        axis=1,
    )
    z_high, z_low = split(CORNER * inv_z.swapaxes(1, 2))
    place = pen ^ jnp.arange(chips, dtype=jnp.int32)

    got = [message(0)]
    for d in range(1, chips):
        got.append(lax.ppermute(message(d), "pen", [(i, i ^ d) for i in range(chips)]))
    middle = chips // 2
    near, y_left, z_high, z_low = lax.optimization_barrier(
        (jnp.stack(got[:middle]), y_left, z_high, z_low)
    )
    far = jnp.stack(got[middle:])

    arrived = [([], []) for _ in range(sections)]
    for value in (near, far):
        for k in range(sections - 1, 0, -1):
            for kind in range(2):
                arrived[k][kind].append(between(value, k, kind == 0))
    for value in (near, far):
        arrived[0][0].append(value)
        arrived[0][1].append(between(value, 0, False))
    head, rest = arrived[-1], arrived[-2::-1]

    fields = jnp.zeros((chips, 2 * height, lanes), F32)
    fields = solve_sections(place, [head], fields, y_left, z_high, z_low)
    fields = solve_sections(place, rest, fields, y_left, z_high, z_low)

    result = jnp.zeros((rhs, 2 * height, lanes), F32)
    for d in range(total):
        piece = lax.dynamic_index_in_dim(fields, pen ^ d, keepdims=False)
        if d > 0:
            pairs = [
                (i * cores + owner(i), (i ^ d) * cores + owner(i)) for i in range(chips)
            ]
            piece = lax.ppermute(piece, ("pen", "rhs"), pairs)
        origin = (pen ^ d) % total
        slot = (jnp.arange(rhs)[:, None, None] == origin % rhs) & (origin // rhs == core)
        result = jnp.where(slot, piece[None], result)
    return result.reshape(rhs, 2, height, lanes).swapaxes(0, 1)[:, :, None]


def solution(mesh):
    return jax.shard_map(
        local,
        mesh=mesh,
        in_specs=(
            P(None, "rhs", "sec", None, "pen"),
            P("sec", None, "pen"),
            P("sec", None, "pen"),
            P("sec", None),
            P(),
            P(),
        ),
        out_specs=P(None, "rhs", "sec", None, "pen"),
        check_vma=False,
    )
```

```python
import functools

import jax
import jax.numpy as jnp
from jax import lax
from jax.experimental import pallas as pl
from jax.experimental.pallas import tpu as pltpu
from jax.sharding import PartitionSpec as P


ITERS = 3
ROWS = 16
SPARE = 2**22
PAD = 8
F32, BF16 = jnp.float32, jnp.bfloat16

CORNER, C, CENTRE = 0.03, 10.0 / 3.0, 1.0 / 3.0
UP, UP_REST = 0.01, 0.05


def halves(value):
    high = value.astype(BF16)
    return high, (value - high.astype(F32)).astype(BF16)


def split(value):
    high = lax.reduce_precision(value, exponent_bits=8, mantissa_bits=7)
    return high.astype(BF16), (value - high).astype(BF16)


def dot(a, b):
    return jnp.dot(a, b, preferred_element_type=F32)


def section_kernel(parted, place, *refs):
    refs = list(refs)
    pieces = [[[refs.pop(0) for _ in range(n)] for _ in range(2)] for n in parted]
    trace, y_left, z_high, z_low, out, res, step, diag, y_in, zh_in, zl_in = refs
    parts, quarters, height, lanes = 2, res.shape[0], diag.shape[2], res.shape[2]
    y_blocks, y_size = y_left.shape[0], y_left.shape[1] // 2
    per_block = z_high.shape[1] // lanes
    chunks = height // ROWS
    lane = lax.broadcasted_iota(jnp.int32, (ROWS, lanes), 1)
    first, last = lane == 0, lane == lanes - 1

    pads = jnp.zeros((PAD, lanes), F32)
    for buffer in range(2):
        for q in range(quarters):
            for c in range(parts):
                step[buffer, q, c, :PAD] = pads
                step[buffer, q, c, PAD + height :] = pads

    def neighbours(buffer, c, base, weight):
        tall = []
        for q in range(quarters):
            here = step[buffer, q, c, pl.ds(PAD + base, ROWS)]
            above = step[buffer, q, c, pl.ds(PAD + base - 1, ROWS)]
            below = step[buffer, q, c, pl.ds(PAD + base + 1, ROWS)]
            tall.append(weight * here + (above + below))
        up = [pltpu.roll(piece, 1, 1) for piece in tall]
        down = [pltpu.roll(piece, lanes - 1, 1) for piece in tall]
        near = []
        for q in range(quarters):
            left = jnp.where(first, up[q - 1] if q > 0 else 0.0, up[q])
            right = jnp.where(last, down[q + 1] if q + 1 < quarters else 0.0, down[q])
            near.append(weight * tall[q] + (left + right))
        return near

    def over_chunks(body):
        def chunk(i, carry):
            body(pl.multiple_of(i * ROWS, ROWS))
            return carry

        lax.fori_loop(0, chunks, chunk, 0, unroll=True)

    def at(arrays, d):
        size = arrays[0].shape[0]
        return arrays[d // size], d % size

    def load(source, diagonal, before, gain):
        for q in range(quarters):
            for c in range(parts):
                step[1, q, c, PAD : PAD + height] = before[q, c * height : (c + 1) * height]
        for d in range(quarters):
            q = place[d]
            array, k = at(source, d)
            res[q] = array[k, : parts * height] * (1.0 / CORNER)
            array, k = at(diagonal, d)
            diag[q, 0] = array[k, :height] * (1.0 / CORNER) + (1.3 + CENTRE) / CORNER
            diag[q, 1] = array[k, height : 2 * height] * (1.0 / CORNER)

        def body(base):
            for c in range(parts):
                rows = pl.ds(c * height + base, ROWS)
                near = neighbours(1, c, base, 3.0)
                for q in range(quarters):
                    here = step[1, q, c, pl.ds(PAD + base, ROWS)]
                    value = res[q, rows] + (UP / CORNER) * near[q] + (UP_REST / CORNER) * here
                    res[q, rows] = value
                    step[0, q, c, pl.ds(PAD + base, ROWS)] = gain * value

        over_chunks(body)

    def apply(source, add, then):
        def body(base):
            near = [neighbours(source, c, base, C) for c in range(parts)]
            for q in range(quarters):
                du = [step[source, q, c, pl.ds(PAD + base, ROWS)] for c in range(parts)]
                real, imag = (diag[q, c, pl.ds(base, ROWS)] for c in range(parts))
                turned = [real * du[0] - imag * du[1], real * du[1] + imag * du[0]]
                for c in range(parts):
                    rows = pl.ds(c * height + base, ROWS)
                    if add is not None:
                        out[q, rows] = add(q, c, base, rows, du[c])
                    value = res[q, rows] - turned[c] + near[c][q]
                    res[q, rows] = value
                    then(q, c, base, rows, value)

        over_chunks(body)

    def for_y(q, c, base, rows, value):
        high, low = halves(value)
        y_in[q, c, 0, pl.ds(base, ROWS)] = high
        y_in[q, c, 1, pl.ds(base, ROWS)] = low

    def for_z(q, c, base, rows, value):
        zh_in[q, rows], zl_in[q, rows] = halves(value)

    def solve_y():
        for b in range(y_blocks):
            rows = slice(b * y_size, (b + 1) * y_size)
            for c in range(parts):
                for q in range(0, quarters, per_block):
                    both = jnp.concatenate(
                        [
                            jnp.concatenate([y_in[q + k, c, h, rows] for h in range(2)], axis=0)
                            for k in range(per_block)
                        ],
                        axis=1,
                    )
                    done = dot(y_left[b], both)
                    done = done[:y_size] + done[y_size:]
                    for k in range(per_block):
                        step[1, q + k, c, PAD + b * y_size : PAD + (b + 1) * y_size] = done[
                            :, k * lanes : (k + 1) * lanes
                        ]

    def solve_z(add):
        for b in range(quarters // per_block):
            span = range(b * per_block, (b + 1) * per_block)
            high = jnp.concatenate([zh_in[q] for q in span], axis=1)
            low = jnp.concatenate([zl_in[q] for q in span], axis=1)
            done = dot(high, z_low[b]) + dot(low, z_high[b]) + dot(high, z_high[b])
            for k, q in enumerate(span):
                piece = done[:, k * lanes : (k + 1) * lanes]
                if add:
                    out[q] += piece
                else:
                    for c in range(parts):
                        step[1, q, c, PAD : PAD + height] = piece[
                            c * height : (c + 1) * height
                        ]

    def solve(source, diagonal, before):
        gain = CORNER * source[0][0, 2 * height, :][None, :]
        load(source, diagonal, before, gain)
        for q in range(quarters):
            out[q] = jnp.zeros(out.shape[1:], F32)

        def for_x(q, c, base, rows, value):
            step[0, q, c, pl.ds(PAD + base, ROWS)] = gain * value

        def two_steps(q, c, base, rows, du):
            return out[q, rows] + (step[0, q, c, pl.ds(PAD + base, ROWS)] + du)

        def one_step(q, c, base, rows, du):
            return out[q, rows] + du

        def sweep(i, carry):
            apply(0, None, for_y)
            solve_y()
            apply(1, two_steps, for_z)

            @pl.when(i + 1 < ITERS)
            def _():
                solve_z(False)
                apply(1, one_step, for_x)

            return carry

        lax.fori_loop(0, ITERS, sweep, 0)
        solve_z(True)

    for index, (source, diagonal) in enumerate(pieces):
        held = place[quarters + index] == 1
        before = trace if index == 0 else out

        @pl.when(held)
        def _(source=source, diagonal=diagonal, before=before):
            solve(source, diagonal, before)

        @pl.when(jnp.logical_not(held))
        def _():
            for q in range(quarters):
                out[q] = jnp.zeros(out.shape[1:], F32)


def solve_sections(place, pieces, trace, y_left, z_high, z_low):
    quarters, rows, lanes = trace.shape
    height = rows // 2
    vmem, smem = (pl.BlockSpec(memory_space=space) for space in (pltpu.VMEM, pltpu.SMEM))
    flat = [array for section in pieces for kind in section for array in kind]
    parted = tuple(len(source) for source, _ in pieces)
    scratch = [
        pltpu.VMEM((quarters, rows, lanes), F32),
        pltpu.VMEM((2, quarters, 2, height + 2 * PAD, lanes), F32),
        pltpu.VMEM((quarters, 2, height, lanes), F32),
        pltpu.VMEM((quarters, 2, 2, height, lanes), BF16),
        pltpu.VMEM((quarters, rows, lanes), BF16),
        pltpu.VMEM((quarters, rows, lanes), BF16),
    ]
    inputs = flat + [trace, y_left, z_high, z_low]
    held = sum(a.size * a.dtype.itemsize for a in inputs + [trace])
    held += 8 * trace.size * trace.dtype.itemsize
    return pl.pallas_call(
        functools.partial(section_kernel, parted),
        out_shape=jax.ShapeDtypeStruct(trace.shape, F32),
        in_specs=[smem] + [vmem] * (len(flat) + 4),
        out_specs=vmem,
        scratch_shapes=scratch,
        compiler_params=pltpu.CompilerParams(vmem_limit_bytes=held + SPARE),
    )(place, *flat, trace, y_left, z_high, z_low)


def local(source, medium, damping, inv_x, inv_y, inv_z):
    rhs, _, height, lanes = source.shape[1:]
    sections, chips, cores = (lax.axis_size(a) for a in ("sec", "pen", "rhs"))
    pen, core = lax.axis_index("pen"), lax.axis_index("rhs")
    total = rhs * cores

    def owner(chip):
        return (chip % total) // rhs

    options = jnp.concatenate(
        [source[:, :, 0].swapaxes(0, 1), jnp.concatenate([medium, damping])[None]]
    ).reshape(rhs + 1, 2 * height, lanes)
    scale = jnp.broadcast_to(inv_x, (8, lanes))

    def message(distance):
        target = pen ^ distance
        pick = jnp.where(owner(target) == core, (target % total) % rhs, rhs)
        body = lax.dynamic_index_in_dim(options, pick, keepdims=False)
        return jnp.concatenate([body, scale])

    def between(value, down, from_owner):
        pairs = []
        for j in range(sections - down):
            for p in range(chips):
                here = owner(p) if from_owner else (owner(p) + 1) % cores
                pairs.append(
                    (
                        (j * chips + p) * cores + here,
                        ((j + down) * chips + p) * cores + owner(p),
                    )
                )
        return lax.ppermute(value, ("sec", "pen", "rhs"), pairs)

    y_high, y_low = split(CORNER * inv_y)
    y_left = jnp.concatenate(
        [jnp.concatenate([y_high, y_high], axis=2), jnp.concatenate([y_low, y_low], axis=2)],
        axis=1,
    )
    z_high, z_low = split(CORNER * inv_z.swapaxes(1, 2))
    section, solver = lax.axis_index("sec"), owner(pen) == core

    def place(downs):
        held = jnp.stack([(section >= k) & solver for k in downs]).astype(jnp.int32)
        return jnp.concatenate([pen ^ jnp.arange(chips, dtype=jnp.int32), held])


    got = [message(0)]
    for d in range(1, chips):
        got.append(lax.ppermute(message(d), "pen", [(i, i ^ d) for i in range(chips)]))
    middle = chips // 2
    near, y_left, z_high, z_low = lax.optimization_barrier(
        (jnp.stack(got[:middle]), y_left, z_high, z_low)
    )
    far = jnp.stack(got[middle:])

    arrived = [([], []) for _ in range(sections)]
    for value in (near, far):
        for k in range(sections - 1, 0, -1):
            for kind in range(2):
                arrived[k][kind].append(between(value, k, kind == 0))
    for value in (near, far):
        arrived[0][0].append(value)
        arrived[0][1].append(between(value, 0, False))

    fields = jnp.zeros((chips, 2 * height, lanes), F32)
    downs = list(range(sections - 1, -1, -1))
    for group in (downs[:1], downs[1:2], downs[2:]):
        if group:
            fields = solve_sections(
                place(group), [arrived[k] for k in group], fields, y_left, z_high, z_low
            )

    result = jnp.zeros((rhs, 2 * height, lanes), F32)
    for d in range(total):
        piece = lax.dynamic_index_in_dim(fields, pen ^ d, keepdims=False)
        if d > 0:
            pairs = [
                (i * cores + owner(i), (i ^ d) * cores + owner(i)) for i in range(chips)
            ]
            piece = lax.ppermute(piece, ("pen", "rhs"), pairs)
        origin = (pen ^ d) % total
        slot = (jnp.arange(rhs)[:, None, None] == origin % rhs) & (origin // rhs == core)
        result = jnp.where(slot, piece[None], result)
    return result.reshape(rhs, 2, height, lanes).swapaxes(0, 1)[:, :, None]


def solution(mesh):
    return jax.shard_map(
        local,
        mesh=mesh,
        in_specs=(
            P(None, "rhs", "sec", None, "pen"),
            P("sec", None, "pen"),
            P("sec", None, "pen"),
            P("sec", None),
            P(),
            P(),
        ),
        out_specs=P(None, "rhs", "sec", None, "pen"),
        check_vma=False,
    )
```

```python
import functools

import jax
import jax.numpy as jnp
from jax import lax
from jax.experimental import pallas as pl
from jax.experimental.pallas import tpu as pltpu
from jax.sharding import PartitionSpec as P


ITERS = 3
ROWS = 16
SPARE = 2**22
PAD = 8
F32, BF16 = jnp.float32, jnp.bfloat16

CORNER, C, CENTRE = 0.03, 10.0 / 3.0, 1.0 / 3.0
UP, UP_REST = 0.01, 0.05


def halves(value):
    high = value.astype(BF16)
    return high, (value - high.astype(F32)).astype(BF16)


def split(value):
    high = lax.reduce_precision(value, exponent_bits=8, mantissa_bits=7)
    return high.astype(BF16), (value - high).astype(BF16)


def y_weights(blocks):
    count, size, _ = blocks.shape
    rows = [
        jnp.concatenate([half, half], axis=2).reshape(count, size // ROWS, ROWS, 2 * size)
        for half in split(blocks)
    ]
    return jnp.stack(rows, axis=2).reshape(count, 2 * size, 2 * size)


def dot(a, b):
    return jnp.dot(a, b, preferred_element_type=F32)


def section_kernel(parted, place, *refs):
    refs = list(refs)
    pieces = [[[refs.pop(0) for _ in range(n)] for _ in range(2)] for n in parted]
    trace, y_left, z_high, z_low, out, res, step, diag, y_in, z_in = refs
    parts, quarters, height, lanes = 2, res.shape[0], diag.shape[2], res.shape[2]
    y_blocks, y_size = y_left.shape[0], y_left.shape[1] // 2
    per_block = z_high.shape[1] // lanes
    chunks = height // ROWS
    lane = lax.broadcasted_iota(jnp.int32, (ROWS, lanes), 1)
    first, last = lane == 0, lane == lanes - 1

    pads = jnp.zeros((PAD, lanes), F32)
    for buffer in range(2):
        for q in range(quarters):
            for c in range(parts):
                step[buffer, q, c, :PAD] = pads
                step[buffer, q, c, PAD + height :] = pads

    def neighbours(buffer, c, base, weight):
        tall = []
        for q in range(quarters):
            here = step[buffer, q, c, pl.ds(PAD + base, ROWS)]
            above = step[buffer, q, c, pl.ds(PAD + base - 1, ROWS)]
            below = step[buffer, q, c, pl.ds(PAD + base + 1, ROWS)]
            tall.append(weight * here + (above + below))
        up = [pltpu.roll(piece, 1, 1) for piece in tall]
        down = [pltpu.roll(piece, lanes - 1, 1) for piece in tall]
        near = []
        for q in range(quarters):
            left = jnp.where(first, up[q - 1] if q > 0 else 0.0, up[q])
            right = jnp.where(last, down[q + 1] if q + 1 < quarters else 0.0, down[q])
            near.append(weight * tall[q] + (left + right))
        return near

    def over_chunks(body):
        def chunk(i, carry):
            body(pl.multiple_of(i * ROWS, ROWS))
            return carry

        lax.fori_loop(0, chunks, chunk, 0, unroll=True)

    def at(arrays, d):
        size = arrays[0].shape[0]
        return arrays[d // size], d % size

    def load(source, diagonal, before, gain):
        for q in range(quarters):
            for c in range(parts):
                step[1, q, c, PAD : PAD + height] = before[q, c * height : (c + 1) * height]
        for d in range(quarters):
            q = place[d]
            array, k = at(source, d)
            res[q] = array[k, : parts * height] * (1.0 / CORNER)
            array, k = at(diagonal, d)
            diag[q, 0] = array[k, :height] * (1.0 / CORNER) + (1.3 + CENTRE) / CORNER
            diag[q, 1] = array[k, height : 2 * height] * (1.0 / CORNER)

        def body(base):
            for c in range(parts):
                rows = pl.ds(c * height + base, ROWS)
                near = neighbours(1, c, base, 3.0)
                for q in range(quarters):
                    here = step[1, q, c, pl.ds(PAD + base, ROWS)]
                    value = res[q, rows] + (UP / CORNER) * near[q] + (UP_REST / CORNER) * here
                    res[q, rows] = value
                    step[0, q, c, pl.ds(PAD + base, ROWS)] = gain * value

        over_chunks(body)

    def apply(source, add, then):
        def body(base):
            near = [neighbours(source, c, base, C) for c in range(parts)]
            for q in range(quarters):
                du = [step[source, q, c, pl.ds(PAD + base, ROWS)] for c in range(parts)]
                real, imag = (diag[q, c, pl.ds(base, ROWS)] for c in range(parts))
                turned = [real * du[0] - imag * du[1], real * du[1] + imag * du[0]]
                for c in range(parts):
                    rows = pl.ds(c * height + base, ROWS)
                    if add is not None:
                        out[q, rows] = add(q, c, base, rows, du[c])
                    value = res[q, rows] - turned[c] + near[c][q]
                    res[q, rows] = value
                    then(q, c, base, rows, value)

        over_chunks(body)

    def for_y(q, c, base, rows, value):
        high, low = halves(value)
        y_in[q, c, 0, pl.ds(base, ROWS)] = high
        y_in[q, c, 1, pl.ds(base, ROWS)] = low

    def for_z(q, c, base, rows, value):
        for h, part in enumerate(halves(value)):
            z_in[q, pl.ds(base * 4 + (2 * h + c) * ROWS, ROWS)] = part

    def solve_y():
        for b in range(y_blocks):
            rows = slice(b * y_size, (b + 1) * y_size)
            for c in range(parts):
                for q in range(0, quarters, per_block):
                    both = jnp.concatenate(
                        [
                            jnp.concatenate([y_in[q + k, c, h, rows] for h in range(2)], axis=0)
                            for k in range(per_block)
                        ],
                        axis=1,
                    )
                    done = dot(y_left[b], both)
                    for i in range(y_size // ROWS):
                        high, low = (
                            done[(2 * i + h) * ROWS : (2 * i + h + 1) * ROWS] for h in range(2)
                        )
                        piece = high + low
                        at = PAD + b * y_size + i * ROWS
                        for k in range(per_block):
                            step[1, q + k, c, at : at + ROWS] = piece[
                                :, k * lanes : (k + 1) * lanes
                            ]

    def solve_z(add):
        for b in range(quarters // per_block):
            span = range(b * per_block, (b + 1) * per_block)
            both = jnp.concatenate([z_in[q] for q in span], axis=1)
            group = 4 * ROWS
            high = jnp.concatenate(
                [both[i * group : i * group + 2 * ROWS] for i in range(chunks)], axis=0
            )
            main, rest = dot(both, z_high[b]), dot(high, z_low[b])
            for i in range(chunks):
                for c in range(parts):
                    piece = rest[(2 * i + c) * ROWS : (2 * i + c + 1) * ROWS]
                    for h in range(2):
                        at = i * group + (2 * h + c) * ROWS
                        piece = piece + main[at : at + ROWS]
                    for k, q in enumerate(span):
                        value = piece[:, k * lanes : (k + 1) * lanes]
                        if add:
                            at = c * height + i * ROWS
                            out[q, at : at + ROWS] += value
                        else:
                            at = PAD + i * ROWS
                            step[1, q, c, at : at + ROWS] = value

    def solve(source, diagonal, before):
        gain = CORNER * source[0][0, 2 * height, :][None, :]
        load(source, diagonal, before, gain)
        for q in range(quarters):
            out[q] = jnp.zeros(out.shape[1:], F32)

        def for_x(q, c, base, rows, value):
            step[0, q, c, pl.ds(PAD + base, ROWS)] = gain * value

        def two_steps(q, c, base, rows, du):
            return out[q, rows] + (step[0, q, c, pl.ds(PAD + base, ROWS)] + du)

        def one_step(q, c, base, rows, du):
            return out[q, rows] + du

        def sweep(i, carry):
            apply(0, None, for_y)
            solve_y()
            apply(1, two_steps, for_z)

            @pl.when(i + 1 < ITERS)
            def _():
                solve_z(False)
                apply(1, one_step, for_x)

            return carry

        lax.fori_loop(0, ITERS, sweep, 0)
        solve_z(True)

    for index, (source, diagonal) in enumerate(pieces):
        held = place[quarters + index] == 1
        before = trace if index == 0 else out

        @pl.when(held)
        def _(source=source, diagonal=diagonal, before=before):
            solve(source, diagonal, before)

        @pl.when(jnp.logical_not(held))
        def _():
            for q in range(quarters):
                out[q] = jnp.zeros(out.shape[1:], F32)


def solve_sections(place, pieces, trace, y_left, z_high, z_low):
    quarters, rows, lanes = trace.shape
    height = rows // 2
    vmem, smem = (pl.BlockSpec(memory_space=space) for space in (pltpu.VMEM, pltpu.SMEM))
    flat = [array for section in pieces for kind in section for array in kind]
    parted = tuple(len(source) for source, _ in pieces)
    scratch = [
        pltpu.VMEM((quarters, rows, lanes), F32),
        pltpu.VMEM((2, quarters, 2, height + 2 * PAD, lanes), F32),
        pltpu.VMEM((quarters, 2, height, lanes), F32),
        pltpu.VMEM((quarters, 2, 2, height, lanes), BF16),
        pltpu.VMEM((quarters, 2 * rows, lanes), BF16),
    ]
    inputs = flat + [trace, y_left, z_high, z_low]
    held = sum(a.size * a.dtype.itemsize for a in inputs + [trace])
    held += 8 * trace.size * trace.dtype.itemsize
    return pl.pallas_call(
        functools.partial(section_kernel, parted),
        out_shape=jax.ShapeDtypeStruct(trace.shape, F32),
        in_specs=[smem] + [vmem] * (len(flat) + 4),
        out_specs=vmem,
        scratch_shapes=scratch,
        compiler_params=pltpu.CompilerParams(vmem_limit_bytes=held + SPARE),
    )(place, *flat, trace, y_left, z_high, z_low)


def local(source, medium, damping, inv_x, inv_y, inv_z):
    rhs, _, height, lanes = source.shape[1:]
    sections, chips, cores = (lax.axis_size(a) for a in ("sec", "pen", "rhs"))
    pen, core = lax.axis_index("pen"), lax.axis_index("rhs")
    total = rhs * cores

    def owner(chip):
        return (chip % total) // rhs

    options = jnp.concatenate(
        [source[:, :, 0].swapaxes(0, 1), jnp.concatenate([medium, damping])[None]]
    ).reshape(rhs + 1, 2 * height, lanes)
    scale = jnp.broadcast_to(inv_x, (8, lanes))

    def message(distance):
        target = pen ^ distance
        pick = jnp.where(owner(target) == core, (target % total) % rhs, rhs)
        body = lax.dynamic_index_in_dim(options, pick, keepdims=False)
        return jnp.concatenate([body, scale])

    def between(value, down, from_owner):
        pairs = []
        for j in range(sections - down):
            for p in range(chips):
                here = owner(p) if from_owner else (owner(p) + 1) % cores
                pairs.append(
                    (
                        (j * chips + p) * cores + here,
                        ((j + down) * chips + p) * cores + owner(p),
                    )
                )
        return lax.ppermute(value, ("sec", "pen", "rhs"), pairs)

    y_left = y_weights(CORNER * inv_y)
    z_high, z_low = split(CORNER * inv_z.swapaxes(1, 2))
    section, solver = lax.axis_index("sec"), owner(pen) == core

    def place(downs):
        held = jnp.stack([(section >= k) & solver for k in downs]).astype(jnp.int32)
        return jnp.concatenate([pen ^ jnp.arange(chips, dtype=jnp.int32), held])


    got = [message(0)]
    for d in range(1, chips):
        got.append(lax.ppermute(message(d), "pen", [(i, i ^ d) for i in range(chips)]))
    middle = chips // 2
    near, y_left, z_high, z_low = lax.optimization_barrier(
        (jnp.stack(got[:middle]), y_left, z_high, z_low)
    )
    far = jnp.stack(got[middle:])

    arrived = [([], []) for _ in range(sections)]
    for value in (near, far):
        for k in range(sections - 1, 0, -1):
            for kind in range(2):
                arrived[k][kind].append(between(value, k, kind == 0))
    for value in (near, far):
        arrived[0][0].append(value)
        arrived[0][1].append(between(value, 0, False))

    fields = jnp.zeros((chips, 2 * height, lanes), F32)
    downs = list(range(sections - 1, -1, -1))
    for group in (downs[:1], downs[1:2], downs[2:]):
        if group:
            fields = solve_sections(
                place(group), [arrived[k] for k in group], fields, y_left, z_high, z_low
            )

    result = jnp.zeros((rhs, 2 * height, lanes), F32)
    for d in range(total):
        piece = lax.dynamic_index_in_dim(fields, pen ^ d, keepdims=False)
        if d > 0:
            pairs = [
                (i * cores + owner(i), (i ^ d) * cores + owner(i)) for i in range(chips)
            ]
            piece = lax.ppermute(piece, ("pen", "rhs"), pairs)
        origin = (pen ^ d) % total
        slot = (jnp.arange(rhs)[:, None, None] == origin % rhs) & (origin // rhs == core)
        result = jnp.where(slot, piece[None], result)
    return result.reshape(rhs, 2, height, lanes).swapaxes(0, 1)[:, :, None]


def solution(mesh):
    return jax.shard_map(
        local,
        mesh=mesh,
        in_specs=(
            P(None, "rhs", "sec", None, "pen"),
            P("sec", None, "pen"),
            P("sec", None, "pen"),
            P("sec", None),
            P(),
            P(),
        ),
        out_specs=P(None, "rhs", "sec", None, "pen"),
        check_vma=False,
    )
```
